32 devices in a mesh: row: 8 (over z, x), col: 4 (over y, core).
Axes of the slice: x: 2, y: 2, z: 4, core: 2. Of those that a mesh axis runs over, the one named last changes fastest.
Arguments:
- sources_in: bfloat16 [32768, 2, 512], P(('row', 'col')), may hold values from -6 to 6
- right_bases: bfloat16 [64, 8, 2, 96, 512], P(('row', 'col')), may hold values from -0.1875 to 0.1875
- left_bases: bfloat16 [8, 8, 8, 2, 96, 512], P('row', None, 'col'), may hold values from -0.046875 to 0.046875
- tile_ranks: int32 [8, 64], P(None, ('row', 'col')), may hold values from 16 to 96
Outputs:
- redatumed: bfloat16 [4096, 2, 512], P(('row', 'col'))
The draws below stay inside these ranges and needn't reach their ends.
Inputs may be any that keep to these rules, and one draw needn't show every extreme that they name: `tile_ranks`: each tile's rank; rows of its bases at or beyond it do not count.
All inputs are finite; a program needn't handle non-finite values.
Results may differ from the reference program's by a relative error of at most 0.0049.
Values may be sent and summed in bfloat16 or wider, within the bound.
A program may use at most 256 MiB of HBM per device.

```python
import jax
import jax.numpy as jnp
from jax import lax

B = 512
RMAX = 96
RMIN = 16
COLS_DEV = 2
S = 512
MT = 8
NT = 64
N_ROW = 8
N_COL = 4


def place_ends(array, stream_key, least, top_value):
    place = [jax.random.randint(jax.random.fold_in(stream_key, axis), (), 0, length) for axis, length in enumerate(array.shape)]
    main_axis = array.shape.index(max(array.shape))
    next_to = place[:main_axis] + [(place[main_axis] + 1) % array.shape[main_axis]] + place[main_axis + 1:]
    return array.at[tuple(place)].set(least).at[tuple(next_to)].set(top_value)


def block_scale(stream_key, shape, split, least, top_value):
    def one(position, parts):
        heights = jax.random.uniform(jax.random.fold_in(jax.random.fold_in(stream_key, 6), position), (parts,), jnp.float32, least / len(split), top_value / len(split))
        return jnp.repeat(jnp.exp(heights), shape[position] // parts).reshape((-1,) + (1,) * (len(shape) - position - 1))

    gain = one(*split[0])
    for cut in split[1:]:
        gain = gain * one(*cut)
    return gain


def normal_values(stream_key, shape, spread, bound, pieces=(), held_as=jnp.bfloat16):
    drawn = spread * jax.random.normal(stream_key, shape, jnp.float32)
    if pieces:
        drawn = drawn * block_scale(stream_key, shape, pieces, -0.22, 0.18)
    return jnp.clip(drawn, -bound, bound).astype(held_as)


def setup_inputs(seed: int = 0) -> dict:
    key_of = jax.random.split(jax.random.key(seed), 5)
    return {
        "sources_in": normal_values(key_of[0], (NT * B, 2, S), 1.0, 6.0, ((0, 32),)),
        "right_bases": normal_values(key_of[1], (NT, MT, 2, RMAX, B), (2 * B) ** -0.5, 0.1875, ((0, 32),)),
        "left_bases": normal_values(key_of[2], (MT, N_ROW, N_COL * COLS_DEV, 2, RMAX, B), (2 * NT * (RMIN + RMAX)) ** -0.5, 0.046875, ((0, 8), (2, 4))),
        "tile_ranks": place_ends(jax.random.randint(key_of[3], (MT, NT), RMIN, RMAX + 1), jax.random.fold_in(key_of[3], 1), RMIN, RMAX).astype(jnp.int32),
    }


def project_column(args):
    basis, block, ranks = args
    right = basis.astype(jnp.float32)
    sources = block.astype(jnp.float32)
    prod = jnp.einsum("mprb,bqs->mpqrs", right, sources)
    real = prod[:, 0, 0] - prod[:, 1, 1]
    imag = prod[:, 0, 1] + prod[:, 1, 0]
    stacked = jnp.stack([real, imag], 1)
    keep = (jnp.arange(RMAX, dtype=jnp.int32)[None, :] < ranks[:, None]).astype(jnp.float32)
    return (stacked * keep[:, None, :, None]).astype(jnp.bfloat16)


def apply_row(args):
    basis, coeffs = args
    left = basis.astype(jnp.float32)
    carried = coeffs.astype(jnp.float32)
    prod = jnp.einsum("jpkb,jqks->bpqs", left, carried)
    real = prod[:, 0, 0] - prod[:, 1, 1]
    imag = prod[:, 0, 1] + prod[:, 1, 0]
    return jnp.stack([real, imag], 1)


def reference(sources_in, right_bases, left_bases, tile_ranks):
    blocks = sources_in.reshape(NT, B, 2, S)
    coeffs = lax.map(project_column, (right_bases, blocks, tile_ranks.T))
    by_rows = jnp.transpose(coeffs, (1, 0, 2, 3, 4))
    left = left_bases.reshape(MT, NT, 2, RMAX, B)
    result = lax.map(apply_row, (left, by_rows))
    return result.reshape(MT * B, 2, S).astype(jnp.bfloat16)
```

```python
import functools

import jax
import jax.numpy as jnp
from jax import lax
from jax.experimental import pallas as pl
from jax.experimental.pallas import tpu as pltpu
from jax.sharding import PartitionSpec as P

MESH = pl.DeviceIdType.MESH
CHUNK = 128


def apply_kernel(
    n_row, n_col, coef, left, out, held, basis, total, outgoing, partial,
    send_sem, recv_sem, psend_sem, precv_sem,
):
    row, col = lax.axis_index("row"), lax.axis_index("col")
    half = n_row // 2
    side = row // half
    place = row % half
    depth, samples = coef.shape[1], coef.shape[2]
    tiles, _, rank_pad, width = left.shape
    cols = tiles // n_row
    chunks = samples // CHUNK
    share = width // n_col

    def to_row(k):
        far = k < half
        there = jnp.where(far, 1 - side, side)
        return there * half + (place + k) % half

    def from_row(k):
        far = k < half
        there = jnp.where(far, 1 - side, side)
        return there * half + (place + 2 * half - k) % half

    steps = [k for k in range(n_row) if k != half]

    barrier = pltpu.get_barrier_semaphore()
    for k in range(1, n_row):
        pl.semaphore_signal(barrier, inc=1, device_id={"row": (row + k) % n_row}, device_id_type=MESH)
    for k in range(1, n_col):
        pl.semaphore_signal(barrier, inc=1, device_id={"col": (col + k) % n_col}, device_id_type=MESH)
    pl.semaphore_wait(barrier, n_row + n_col - 2)

    def coef_copy(k, dest, slot, ch):
        lanes = pl.ds(ch * CHUNK, CHUNK)
        return pltpu.make_async_remote_copy(
            src_ref=coef.at[dest, :, lanes],
            dst_ref=held.at[slot, :, lanes],
            send_sem=send_sem.at[k, ch],
            recv_sem=recv_sem.at[k, ch],
            device_id={"row": dest},
            device_id_type=MESH,
        )

    for ch in range(chunks):
        for k in steps:
            coef_copy(k, to_row(k), row, ch).start()

    def prepare(a, carry):
        plain, swapped = [], []
        for c in range(cols):
            real, imag = left[a * cols + c, 0], left[a * cols + c, 1]
            plain += [real, -imag]
            swapped += [imag, real]
        basis[a, 0:width, :] = jnp.concatenate(plain, 0).T
        basis[a, width : 2 * width, :] = jnp.concatenate(swapped, 0).T
        return carry

    lax.fori_loop(0, n_row, prepare, 0)

    def partial_copy(k, ch):
        dest = (col + k) % n_col
        return pltpu.make_async_remote_copy(
            src_ref=outgoing.at[ch, :, pl.ds(pl.multiple_of(dest * share, share), share)],
            dst_ref=partial.at[ch, k - 1],
            send_sem=psend_sem.at[k, ch],
            recv_sem=precv_sem.at[k, ch],
            device_id={"col": dest},
            device_id_type=MESH,
        )

    def finish(ch):
        lanes = pl.ds(ch * CHUNK, CHUNK)
        mine = outgoing[ch, :, pl.ds(pl.multiple_of(col * share, share), share), :]
        for k in range(1, n_col):
            partial_copy(k, ch).wait_recv()
            mine = mine + partial[ch, k - 1]
        out[:, :, lanes] = mine.astype(out.dtype)

    for ch in range(chunks):
        lanes = pl.ds(ch * CHUNK, CHUNK)
        total[...] = jnp.dot(basis[row], coef[row, :, lanes], preferred_element_type=jnp.float32)

        def take(k, carry):
            source = from_row(k)
            coef_copy(k, to_row(k), source, ch).wait_recv()
            total[...] += jnp.dot(basis[source], held[source, :, lanes], preferred_element_type=jnp.float32)
            return carry

        lax.fori_loop(half + 1, n_row, take, 0)
        lax.fori_loop(0, half, take, 0)
        outgoing[ch] = total[...].reshape(2, width, CHUNK)
        for k in range(1, n_col):
            partial_copy(k, ch).start()
        if ch > 0:
            finish(ch - 1)
    finish(chunks - 1)
    for ch in range(chunks):
        for k in steps:
            coef_copy(k, to_row(k), row, ch).wait_send()
        for k in range(1, n_col):
            partial_copy(k, ch).wait_send()


def body(n_row, n_col, sources_in, right_bases, left_bases, tile_ranks):
    cols, tile_rows, _, rank_pad, width = right_bases.shape
    samples = sources_in.shape[2]
    blocks = sources_in.reshape(cols, width, 2, samples)
    prod = jnp.einsum("cmprb,cbqs->cmpqrs", right_bases, blocks, preferred_element_type=jnp.float32)
    real = prod[:, :, 0, 0] - prod[:, :, 1, 1]
    imag = prod[:, :, 0, 1] + prod[:, :, 1, 0]
    levels = lax.broadcasted_iota(jnp.int32, (cols, tile_rows, rank_pad), 2)
    keep = (levels < tile_ranks.T[:, :, None]).astype(jnp.float32)
    coeffs = (jnp.stack([real, imag], 2) * keep[:, :, None, :, None]).astype(jnp.bfloat16)
    depth = cols * 2 * rank_pad
    coeffs = coeffs.transpose(1, 0, 2, 3, 4).reshape(tile_rows, depth, samples)
    left = left_bases.reshape(-1, 2, rank_pad, width)
    chunks = samples // CHUNK
    share = width // n_col
    vmem = pl.BlockSpec(memory_space=pltpu.VMEM)
    out = pl.pallas_call(
        functools.partial(apply_kernel, n_row, n_col),
        out_shape=jax.ShapeDtypeStruct((2, share, samples), jnp.bfloat16),
        in_specs=[vmem, vmem],
        out_specs=vmem,
        scratch_shapes=[
            pltpu.VMEM((n_row, depth, samples), jnp.bfloat16),
            pltpu.VMEM((n_row, 2 * width, depth), jnp.bfloat16),
            pltpu.VMEM((2 * width, CHUNK), jnp.float32),
            pltpu.VMEM((chunks, 2, width, CHUNK), jnp.float32),
            pltpu.VMEM((chunks, n_col - 1, 2, share, CHUNK), jnp.float32),
            pltpu.SemaphoreType.DMA((n_row, chunks)),
            pltpu.SemaphoreType.DMA((n_row, chunks)),
            pltpu.SemaphoreType.DMA((n_col, chunks)),
            pltpu.SemaphoreType.DMA((n_col, chunks)),
        ],
        compiler_params=pltpu.CompilerParams(
            collective_id=0, has_side_effects=True, vmem_limit_bytes=56 * 2**20
        ),
    )(coeffs, left)
    return out.transpose(1, 0, 2)


def solution(mesh):
    in_specs = (
        P(("row", "col"), None, None),
        P(("row", "col"), None, None, None, None),
        P("row", None, "col", None, None, None),
        P(None, ("row", "col")),
    )
    return jax.shard_map(
        functools.partial(body, mesh.shape["row"], mesh.shape["col"]),
        mesh=mesh,
        in_specs=in_specs,
        out_specs=P(("row", "col"), None, None),
        check_vma=False,
    )
```

```python
import functools

import jax
import jax.numpy as jnp
from jax import lax
from jax.experimental import pallas as pl
from jax.experimental.pallas import tpu as pltpu
from jax.sharding import PartitionSpec as P

MESH = pl.DeviceIdType.MESH
CHUNK = 128


def apply_kernel(
    n_row, n_col, ranks, sources, right, left_in, out, block, bases, left, split, coef, held,
    basis, total, outgoing, partial,
    load_sem, send_sem, recv_sem, psend_sem, precv_sem,
):
    row, col = lax.axis_index("row"), lax.axis_index("col")
    half = n_row // 2
    side = row // half
    place = row % half
    samples = coef.shape[2]
    tiles, _, rank_pad, width = left.shape
    cols = tiles // n_row
    chunks = samples // CHUNK
    share = width // n_col
    pair = 2 * rank_pad
    step_rows = 2 * CHUNK

    loads = [
        pltpu.make_async_copy(
            sources.at[pl.ds(c * width, width)], block.at[pl.ds(c * width, width)], load_sem.at[c]
        )
        for c in range(cols)
    ]
    loads.append(pltpu.make_async_copy(right, bases, load_sem.at[cols]))
    loads.append(pltpu.make_async_copy(left_in, left, load_sem.at[cols + 1]))
    for load in loads:
        load.start()

    def to_row(k):
        far = k < half
        there = jnp.where(far, 1 - side, side)
        return there * half + (place + k) % half

    def from_row(k):
        far = k < half
        there = jnp.where(far, 1 - side, side)
        return there * half + (place + 2 * half - k) % half

    steps = [k for k in range(n_row) if k != half]

    barrier = pltpu.get_barrier_semaphore()
    for k in range(1, n_row):
        pl.semaphore_signal(barrier, inc=1, device_id={"row": (row + k) % n_row}, device_id_type=MESH)
    for k in range(1, n_col):
        pl.semaphore_signal(barrier, inc=1, device_id={"col": (col + k) % n_col}, device_id_type=MESH)
    pl.semaphore_wait(barrier, n_row + n_col - 2)

    def coef_copy(k, dest, slot, ch):
        lanes = pl.ds(ch * CHUNK, CHUNK)
        return pltpu.make_async_remote_copy(
            src_ref=coef.at[dest, :, lanes],
            dst_ref=held.at[slot, :, lanes],
            send_sem=send_sem.at[k, ch],
            recv_sem=recv_sem.at[k, ch],
            device_id={"row": dest},
            device_id_type=MESH,
        )

    at = lax.broadcasted_iota(jnp.int32, (step_rows, step_rows), 0)
    picked = jnp.where(at < CHUNK, 2 * at, 2 * (at - CHUNK) + 1)
    unweave = jnp.where(lax.broadcasted_iota(jnp.int32, (step_rows, step_rows), 1) == picked, 1.0, 0.0)
    unweave = unweave.astype(jnp.bfloat16)
    levels = lax.broadcasted_iota(jnp.int32, (rank_pad, CHUNK), 0)
    woven = block.reshape(2 * cols * width, samples)

    def project(dest, lanes):
        for c in range(cols):
            prod = jnp.dot(bases[c, dest], split[c], preferred_element_type=jnp.float32)
            real = prod[:rank_pad, :CHUNK] - prod[rank_pad:, CHUNK:]
            imag = prod[:rank_pad, CHUNK:] + prod[rank_pad:, :CHUNK]
            keep = levels < ranks[c, dest]
            coef[dest, c * pair : c * pair + rank_pad, lanes] = jnp.where(keep, real, 0.0).astype(coef.dtype)
            coef[dest, c * pair + rank_pad : (c + 1) * pair, lanes] = jnp.where(keep, imag, 0.0).astype(coef.dtype)

    for ch in range(chunks):
        lanes = pl.ds(ch * CHUNK, CHUNK)
        for c in range(cols):
            if ch == 0:
                loads[c].wait()
            for t in range(width // CHUNK):
                rows = woven[pl.ds(2 * (c * width + t * CHUNK), step_rows), lanes]
                apart = jnp.dot(unweave, rows, preferred_element_type=jnp.float32).astype(split.dtype)
                split[c, t * CHUNK : (t + 1) * CHUNK, :CHUNK] = apart[:CHUNK]
                split[c, t * CHUNK : (t + 1) * CHUNK, CHUNK:] = apart[CHUNK:]
        if ch == 0:
            loads[cols].wait()

        def project_send(k, carry):
            dest = to_row(k)
            project(dest, lanes)
            coef_copy(k, dest, row, ch).start()
            return carry

        lax.fori_loop(0, half, project_send, 0)
        lax.fori_loop(half + 1, n_row, project_send, 0)
        project(row, lanes)
    loads[cols + 1].wait()

    def prepare(a, carry):
        plain, swapped = [], []
        for c in range(cols):
            real, imag = left[a * cols + c, 0], left[a * cols + c, 1]
            plain += [real, -imag]
            swapped += [imag, real]
        basis[a, 0:width, :] = jnp.concatenate(plain, 0).T
        basis[a, width : 2 * width, :] = jnp.concatenate(swapped, 0).T
        return carry

    lax.fori_loop(0, n_row, prepare, 0)

    def partial_copy(k, ch):
        dest = (col + k) % n_col
        return pltpu.make_async_remote_copy(
            src_ref=outgoing.at[ch, :, pl.ds(pl.multiple_of(dest * share, share), share)],
            dst_ref=partial.at[ch, k - 1],
            send_sem=psend_sem.at[k, ch],
            recv_sem=precv_sem.at[k, ch],
            device_id={"col": dest},
            device_id_type=MESH,
        )

    def finish(ch):
        lanes = pl.ds(ch * CHUNK, CHUNK)
        mine = outgoing[ch, :, pl.ds(pl.multiple_of(col * share, share), share), :]
        for k in range(1, n_col):
            partial_copy(k, ch).wait_recv()
            mine = mine + partial[ch, k - 1]
        out[:, :, lanes] = mine.astype(out.dtype)

    for ch in range(chunks):
        lanes = pl.ds(ch * CHUNK, CHUNK)
        total[...] = jnp.dot(basis[row], coef[row, :, lanes], preferred_element_type=jnp.float32)

        def take(k, carry):
            source = from_row(k)
            coef_copy(k, to_row(k), source, ch).wait_recv()
            total[...] += jnp.dot(basis[source], held[source, :, lanes], preferred_element_type=jnp.float32)
            return carry

        lax.fori_loop(half + 1, n_row, take, 0)
        lax.fori_loop(0, half, take, 0)
        outgoing[ch] = total[...].reshape(2, width, CHUNK)
        for k in range(1, n_col):
            partial_copy(k, ch).start()
        if ch > 0:
            finish(ch - 1)
    finish(chunks - 1)
    for ch in range(chunks):
        for k in steps:
            coef_copy(k, to_row(k), row, ch).wait_send()
        for k in range(1, n_col):
            partial_copy(k, ch).wait_send()


def body(n_row, n_col, sources_in, right_bases, left_bases, tile_ranks):
    cols, tile_rows, _, rank_pad, width = right_bases.shape
    samples = sources_in.shape[2]
    depth = cols * 2 * rank_pad
    right = right_bases.reshape(cols, tile_rows, 2 * rank_pad, width)
    left = left_bases.reshape(-1, 2, rank_pad, width)
    chunks = samples // CHUNK
    share = width // n_col
    vmem = pl.BlockSpec(memory_space=pltpu.VMEM)
    out = pl.pallas_call(
        functools.partial(apply_kernel, n_row, n_col),
        out_shape=jax.ShapeDtypeStruct((2, share, samples), jnp.bfloat16),
        in_specs=[pl.BlockSpec(memory_space=pltpu.SMEM)] + [pl.BlockSpec(memory_space=pl.ANY)] * 3,
        out_specs=vmem,
        scratch_shapes=[
            pltpu.VMEM(sources_in.shape, jnp.bfloat16),
            pltpu.VMEM(right.shape, jnp.bfloat16),
            pltpu.VMEM(left.shape, jnp.bfloat16),
            pltpu.VMEM((cols, width, 2 * CHUNK), jnp.bfloat16),
            pltpu.VMEM((n_row, depth, samples), jnp.bfloat16),
            pltpu.VMEM((n_row, depth, samples), jnp.bfloat16),
            pltpu.VMEM((n_row, 2 * width, depth), jnp.bfloat16),
            pltpu.VMEM((2 * width, CHUNK), jnp.float32),
            pltpu.VMEM((chunks, 2, width, CHUNK), jnp.float32),
            pltpu.VMEM((chunks, n_col - 1, 2, share, CHUNK), jnp.float32),
            pltpu.SemaphoreType.DMA((cols + 2,)),
            pltpu.SemaphoreType.DMA((n_row, chunks)),
            pltpu.SemaphoreType.DMA((n_row, chunks)),
            pltpu.SemaphoreType.DMA((n_col, chunks)),
            pltpu.SemaphoreType.DMA((n_col, chunks)),
        ],
        compiler_params=pltpu.CompilerParams(
            collective_id=0, has_side_effects=True, vmem_limit_bytes=56 * 2**20
        ),
    )(tile_ranks.T, sources_in, right, left)
    return out.transpose(1, 0, 2)


def solution(mesh):
    in_specs = (
        P(("row", "col"), None, None),
        P(("row", "col"), None, None, None, None),
        P("row", None, "col", None, None, None),
        P(None, ("row", "col")),
    )
    return jax.shard_map(
        functools.partial(body, mesh.shape["row"], mesh.shape["col"]),
        mesh=mesh,
        in_specs=in_specs,
        out_specs=P(("row", "col"), None, None),
        check_vma=False,
    )
```

```python
import functools

import jax
import jax.numpy as jnp
from jax import lax
from jax.experimental import pallas as pl
from jax.experimental.pallas import tpu as pltpu
from jax.sharding import PartitionSpec as P

MESH = pl.DeviceIdType.MESH
CHUNK = 128


def apply_kernel(
    n_row, n_col, ranks, sources, right, left_in, out, block, bases, left, split, coef, held,
    basis, total, own, outgoing, partial,
    load_sem, send_sem, recv_sem, psend_sem, precv_sem,
):
    row, col = lax.axis_index("row"), lax.axis_index("col")
    half = n_row // 2
    side = row // half
    place = row % half
    samples = coef.shape[2]
    tiles, _, rank_pad, width = left.shape
    cols = tiles // n_row
    chunks = samples // CHUNK
    share = width // n_col
    pair = 2 * rank_pad
    step_rows = 2 * CHUNK

    loads = [
        pltpu.make_async_copy(
            sources.at[pl.ds(c * width, width)], block.at[pl.ds(c * width, width)], load_sem.at[c]
        )
        for c in range(cols)
    ]
    loads.append(pltpu.make_async_copy(right, bases, load_sem.at[cols]))
    loads.append(pltpu.make_async_copy(left_in, left, load_sem.at[cols + 1]))
    for load in loads:
        load.start()

    def to_row(k):
        far = k < half
        there = jnp.where(far, 1 - side, side)
        return there * half + (place + k) % half

    def from_row(k):
        far = k < half
        there = jnp.where(far, 1 - side, side)
        return there * half + (place + 2 * half - k) % half

    steps = [k for k in range(n_row) if k != half]

    barrier = pltpu.get_barrier_semaphore()
    for k in range(1, n_row):
        pl.semaphore_signal(barrier, inc=1, device_id={"row": (row + k) % n_row}, device_id_type=MESH)
    for k in range(1, n_col):
        pl.semaphore_signal(barrier, inc=1, device_id={"col": (col + k) % n_col}, device_id_type=MESH)

    def coef_copy(k, dest, slot, ch):
        lanes = pl.ds(ch * CHUNK, CHUNK)
        return pltpu.make_async_remote_copy(
            src_ref=coef.at[dest, :, lanes],
            dst_ref=held.at[slot, :, lanes],
            send_sem=send_sem.at[k, ch],
            recv_sem=recv_sem.at[k, ch],
            device_id={"row": dest},
            device_id_type=MESH,
        )

    at = lax.broadcasted_iota(jnp.int32, (step_rows, step_rows), 0)
    picked = jnp.where(at < CHUNK, 2 * at, 2 * (at - CHUNK) + 1)
    unweave = jnp.where(lax.broadcasted_iota(jnp.int32, (step_rows, step_rows), 1) == picked, 1.0, 0.0)
    unweave = unweave.astype(jnp.bfloat16)
    levels = lax.broadcasted_iota(jnp.int32, (rank_pad, CHUNK), 0)
    woven = block.reshape(2 * cols * width, samples)

    def project(dest, lanes):
        for c in range(cols):
            prod = jnp.dot(bases[c, dest], split[c], preferred_element_type=jnp.float32)
            real = prod[:rank_pad, :CHUNK] - prod[rank_pad:, CHUNK:]
            imag = prod[:rank_pad, CHUNK:] + prod[rank_pad:, :CHUNK]
            keep = levels < ranks[c, dest]
            coef[dest, c * pair : c * pair + rank_pad, lanes] = jnp.where(keep, real, 0.0).astype(coef.dtype)
            coef[dest, c * pair + rank_pad : (c + 1) * pair, lanes] = jnp.where(keep, imag, 0.0).astype(coef.dtype)

    for ch in range(chunks):
        lanes = pl.ds(ch * CHUNK, CHUNK)
        for c in range(cols):
            if ch == 0:
                loads[c].wait()
            for t in range(width // CHUNK):
                rows = woven[pl.ds(2 * (c * width + t * CHUNK), step_rows), lanes]
                apart = jnp.dot(unweave, rows, preferred_element_type=jnp.float32).astype(split.dtype)
                split[c, t * CHUNK : (t + 1) * CHUNK, :CHUNK] = apart[:CHUNK]
                split[c, t * CHUNK : (t + 1) * CHUNK, CHUNK:] = apart[CHUNK:]
        if ch == 0:
            loads[cols].wait()
            pl.semaphore_wait(barrier, n_row + n_col - 2)

        def project_send(k, carry):
            dest = to_row(k)
            project(dest, lanes)
            coef_copy(k, dest, row, ch).start()
            return carry

        lax.fori_loop(0, half, project_send, 0)
        lax.fori_loop(half + 1, n_row, project_send, 0)
        project(row, lanes)
    loads[cols + 1].wait()

    def prepare(a, carry):
        plain, swapped = [], []
        for c in range(cols):
            real, imag = left[a * cols + c, 0], left[a * cols + c, 1]
            plain += [real, -imag]
            swapped += [imag, real]
        basis[a, 0:width, :] = jnp.concatenate(plain, 0).T
        basis[a, width : 2 * width, :] = jnp.concatenate(swapped, 0).T
        return carry

    lax.fori_loop(0, n_row, prepare, 0)

    def partial_copy(k, ch):
        dest = (col + k) % n_col
        return pltpu.make_async_remote_copy(
            src_ref=outgoing.at[ch, :, pl.ds(pl.multiple_of(dest * share, share), share)],
            dst_ref=partial.at[ch, k - 1],
            send_sem=psend_sem.at[k, ch],
            recv_sem=precv_sem.at[k, ch],
            device_id={"col": dest},
            device_id_type=MESH,
        )

    to = lax.broadcasted_iota(jnp.int32, (2 * share, 2 * share), 0)
    near = lax.broadcasted_iota(jnp.int32, (2 * share, 2 * share), 1)
    weave = jnp.where(to == jnp.where(near < share, 2 * near, 2 * (near - share) + 1), 1.0, 0.0)
    weave = weave.astype(jnp.bfloat16)
    result = out.reshape(2 * share, samples)

    def finish(ch):
        mine = own[ch]
        for k in range(1, n_col):
            partial_copy(k, ch).wait_recv()
            mine = mine + partial[ch, k - 1].astype(jnp.float32)
        rounded = mine.astype(out.dtype).reshape(2 * share, CHUNK)
        woven_out = jnp.dot(weave, rounded, preferred_element_type=jnp.float32)
        result[:, pl.ds(ch * CHUNK, CHUNK)] = woven_out.astype(out.dtype)

    for ch in range(chunks):
        lanes = pl.ds(ch * CHUNK, CHUNK)
        total[...] = jnp.dot(basis[row], coef[row, :, lanes], preferred_element_type=jnp.float32)

        def take(k, carry):
            source = from_row(k)
            coef_copy(k, to_row(k), source, ch).wait_recv()
            total[...] += jnp.dot(basis[source], held[source, :, lanes], preferred_element_type=jnp.float32)
            return carry

        lax.fori_loop(half + 1, n_row, take, 0)
        lax.fori_loop(0, half, take, 0)
        outgoing[ch] = total[...].reshape(2, width, CHUNK).astype(outgoing.dtype)
        for q in range(2):
            own[ch, q] = total[pl.ds(pl.multiple_of(q * width + col * share, share), share)]
        for k in range(1, n_col):
            partial_copy(k, ch).start()
        if ch > 0:
            finish(ch - 1)
    finish(chunks - 1)
    for ch in range(chunks):
        for k in steps:
            coef_copy(k, to_row(k), row, ch).wait_send()
        for k in range(1, n_col):
            partial_copy(k, ch).wait_send()


def body(n_row, n_col, sources_in, right_bases, left_bases, tile_ranks):
    cols, tile_rows, _, rank_pad, width = right_bases.shape
    samples = sources_in.shape[2]
    depth = cols * 2 * rank_pad
    right = right_bases.reshape(cols, tile_rows, 2 * rank_pad, width)
    left = left_bases.reshape(-1, 2, rank_pad, width)
    chunks = samples // CHUNK
    share = width // n_col
    vmem = pl.BlockSpec(memory_space=pltpu.VMEM)
    return pl.pallas_call(
        functools.partial(apply_kernel, n_row, n_col),
        out_shape=jax.ShapeDtypeStruct((share, 2, samples), jnp.bfloat16),
        in_specs=[pl.BlockSpec(memory_space=pltpu.SMEM)] + [pl.BlockSpec(memory_space=pl.ANY)] * 3,
        out_specs=vmem,
        scratch_shapes=[
            pltpu.VMEM(sources_in.shape, jnp.bfloat16),
            pltpu.VMEM(right.shape, jnp.bfloat16),
            pltpu.VMEM(left.shape, jnp.bfloat16),
            pltpu.VMEM((cols, width, 2 * CHUNK), jnp.bfloat16),
            pltpu.VMEM((n_row, depth, samples), jnp.bfloat16),
            pltpu.VMEM((n_row, depth, samples), jnp.bfloat16),
            pltpu.VMEM((n_row, 2 * width, depth), jnp.bfloat16),
            pltpu.VMEM((2 * width, CHUNK), jnp.float32),
            pltpu.VMEM((chunks, 2, share, CHUNK), jnp.float32),
            pltpu.VMEM((chunks, 2, width, CHUNK), jnp.bfloat16),
            pltpu.VMEM((chunks, n_col - 1, 2, share, CHUNK), jnp.bfloat16),
            pltpu.SemaphoreType.DMA((cols + 2,)),
            pltpu.SemaphoreType.DMA((n_row, chunks)),
            pltpu.SemaphoreType.DMA((n_row, chunks)),
            pltpu.SemaphoreType.DMA((n_col, chunks)),
            pltpu.SemaphoreType.DMA((n_col, chunks)),
        ],
        compiler_params=pltpu.CompilerParams(
            collective_id=0, has_side_effects=True, vmem_limit_bytes=56 * 2**20
        ),
    )(tile_ranks.T, sources_in, right, left)


def solution(mesh):
    in_specs = (
        P(("row", "col"), None, None),
        P(("row", "col"), None, None, None, None),
        P("row", None, "col", None, None, None),
        P(None, ("row", "col")),
    )
    return jax.shard_map(
        functools.partial(body, mesh.shape["row"], mesh.shape["col"]),
        mesh=mesh,
        in_specs=in_specs,
        out_specs=P(("row", "col"), None, None),
        check_vma=False,
    )
```

```python
import functools

import jax
import jax.numpy as jnp
from jax import lax
from jax.experimental import pallas as pl
from jax.experimental.pallas import tpu as pltpu
from jax.sharding import PartitionSpec as P

MESH = pl.DeviceIdType.MESH
CHUNK = 128


def apply_kernel(
    n_row, n_col, ranks, sources, right, left_in, out, block, bases, left, split, coef, held,
    basis, total, own, outgoing, partial,
    load_sem, send_sem, recv_sem, psend_sem, precv_sem,
):
    row, col = lax.axis_index("row"), lax.axis_index("col")
    half = n_row // 2
    side = row // half
    place = row % half
    samples = coef.shape[2]
    tiles, _, rank_pad, width = left.shape
    cols = tiles // n_row
    chunks = samples // CHUNK
    share = width // n_col
    pair = 2 * rank_pad
    step_rows = 2 * CHUNK

    def load_part(ch):
        lanes = pl.ds(ch * CHUNK, CHUNK)
        return pltpu.make_async_copy(sources.at[:, :, lanes], block.at[:, :, lanes], load_sem.at[ch])

    def load_bases(there, at):
        span = pl.ds(there * half, half)
        return pltpu.make_async_copy(right.at[:, span], bases.at[:, span], load_sem.at[chunks + at])

    far_bases, near_bases = load_bases(1 - side, 0), load_bases(side, 1)
    load_left = pltpu.make_async_copy(left_in, left, load_sem.at[chunks + 2])
    load_part(0).start()
    far_bases.start()

    def to_row(k):
        far = k < half
        there = jnp.where(far, 1 - side, side)
        return there * half + (place + k) % half

    def from_row(k):
        far = k < half
        there = jnp.where(far, 1 - side, side)
        return there * half + (place + 2 * half - k) % half

    steps = [k for k in range(n_row) if k != half]

    barrier = pltpu.get_barrier_semaphore()
    for k in range(1, n_row):
        pl.semaphore_signal(barrier, inc=1, device_id={"row": (row + k) % n_row}, device_id_type=MESH)
    for k in range(1, n_col):
        pl.semaphore_signal(barrier, inc=1, device_id={"col": (col + k) % n_col}, device_id_type=MESH)

    def coef_copy(k, dest, slot, ch):
        lanes = pl.ds(ch * CHUNK, CHUNK)
        return pltpu.make_async_remote_copy(
            src_ref=coef.at[dest, :, lanes],
            dst_ref=held.at[slot, :, lanes],
            send_sem=send_sem.at[k, ch],
            recv_sem=recv_sem.at[k, ch],
            device_id={"row": dest},
            device_id_type=MESH,
        )

    at = lax.broadcasted_iota(jnp.int32, (step_rows, step_rows), 0)
    picked = jnp.where(at < CHUNK, 2 * at, 2 * (at - CHUNK) + 1)
    unweave = jnp.where(lax.broadcasted_iota(jnp.int32, (step_rows, step_rows), 1) == picked, 1.0, 0.0)
    unweave = unweave.astype(jnp.bfloat16)
    levels = lax.broadcasted_iota(jnp.int32, (rank_pad, CHUNK), 0)
    woven = block.reshape(2 * cols * width, samples)

    def project(dest, lanes):
        for c in range(cols):
            prod = jnp.dot(bases[c, dest], split[c], preferred_element_type=jnp.float32)
            real = prod[:rank_pad, :CHUNK] - prod[rank_pad:, CHUNK:]
            imag = prod[:rank_pad, CHUNK:] + prod[rank_pad:, :CHUNK]
            keep = levels < ranks[c, dest]
            coef[dest, c * pair : c * pair + rank_pad, lanes] = jnp.where(keep, real, 0.0).astype(coef.dtype)
            coef[dest, c * pair + rank_pad : (c + 1) * pair, lanes] = jnp.where(keep, imag, 0.0).astype(coef.dtype)

    for ch in range(chunks):
        lanes = pl.ds(ch * CHUNK, CHUNK)
        for c in range(cols):
            if c == 0:
                load_part(ch).wait()
            for t in range(width // CHUNK):
                rows = woven[pl.ds(2 * (c * width + t * CHUNK), step_rows), lanes]
                apart = jnp.dot(unweave, rows, preferred_element_type=jnp.float32).astype(split.dtype)
                split[c, t * CHUNK : (t + 1) * CHUNK, :CHUNK] = apart[:CHUNK]
                split[c, t * CHUNK : (t + 1) * CHUNK, CHUNK:] = apart[CHUNK:]
        if ch == 0:
            far_bases.wait()
            near_bases.start()
            for later in range(1, chunks):
                load_part(later).start()
            load_left.start()
            pl.semaphore_wait(barrier, n_row + n_col - 2)

        def project_send(k, carry):
            dest = to_row(k)
            project(dest, lanes)
            coef_copy(k, dest, row, ch).start()
            return carry

        lax.fori_loop(0, half, project_send, 0)
        if ch == 0:
            near_bases.wait()
        lax.fori_loop(half + 1, n_row, project_send, 0)
        project(row, lanes)
    load_left.wait()

    def prepare(a, carry):
        plain, swapped = [], []
        for c in range(cols):
            real, imag = left[a * cols + c, 0], left[a * cols + c, 1]
            plain += [real, -imag]
            swapped += [imag, real]
        basis[a, 0:width, :] = jnp.concatenate(plain, 0).T
        basis[a, width : 2 * width, :] = jnp.concatenate(swapped, 0).T
        return carry

    lax.fori_loop(0, n_row, prepare, 0)

    def partial_copy(k, ch):
        dest = (col + k) % n_col
        return pltpu.make_async_remote_copy(
            src_ref=outgoing.at[ch, :, pl.ds(pl.multiple_of(dest * share, share), share)],
            dst_ref=partial.at[ch, k - 1],
            send_sem=psend_sem.at[k, ch],
            recv_sem=precv_sem.at[k, ch],
            device_id={"col": dest},
            device_id_type=MESH,
        )

    to = lax.broadcasted_iota(jnp.int32, (2 * share, 2 * share), 0)
    near = lax.broadcasted_iota(jnp.int32, (2 * share, 2 * share), 1)
    weave = jnp.where(to == jnp.where(near < share, 2 * near, 2 * (near - share) + 1), 1.0, 0.0)
    weave = weave.astype(jnp.bfloat16)
    result = out.reshape(2 * share, samples)

    def finish(ch):
        mine = own[ch]
        for k in range(1, n_col):
            partial_copy(k, ch).wait_recv()
            mine = mine + partial[ch, k - 1].astype(jnp.float32)
        rounded = mine.astype(out.dtype).reshape(2 * share, CHUNK)
        woven_out = jnp.dot(weave, rounded, preferred_element_type=jnp.float32)
        result[:, pl.ds(ch * CHUNK, CHUNK)] = woven_out.astype(out.dtype)

    for ch in range(chunks):
        lanes = pl.ds(ch * CHUNK, CHUNK)
        total[...] = jnp.dot(basis[row], coef[row, :, lanes], preferred_element_type=jnp.float32)

        def take(k, carry):
            source = from_row(k)
            coef_copy(k, to_row(k), source, ch).wait_recv()
            total[...] += jnp.dot(basis[source], held[source, :, lanes], preferred_element_type=jnp.float32)
            return carry

        lax.fori_loop(half + 1, n_row, take, 0)
        lax.fori_loop(0, half, take, 0)
        outgoing[ch] = total[...].reshape(2, width, CHUNK).astype(outgoing.dtype)
        for q in range(2):
            own[ch, q] = total[pl.ds(pl.multiple_of(q * width + col * share, share), share)]
        for k in range(1, n_col):
            partial_copy(k, ch).start()
        if ch > 0:
            finish(ch - 1)
    finish(chunks - 1)
    for ch in range(chunks):
        for k in steps:
            coef_copy(k, to_row(k), row, ch).wait_send()
        for k in range(1, n_col):
            partial_copy(k, ch).wait_send()


def body(n_row, n_col, sources_in, right_bases, left_bases, tile_ranks):
    cols, tile_rows, _, rank_pad, width = right_bases.shape
    samples = sources_in.shape[2]
    depth = cols * 2 * rank_pad
    right = right_bases.reshape(cols, tile_rows, 2 * rank_pad, width)
    left = left_bases.reshape(-1, 2, rank_pad, width)
    chunks = samples // CHUNK
    share = width // n_col
    vmem = pl.BlockSpec(memory_space=pltpu.VMEM)
    return pl.pallas_call(
        functools.partial(apply_kernel, n_row, n_col),
        out_shape=jax.ShapeDtypeStruct((share, 2, samples), jnp.bfloat16),
        in_specs=[pl.BlockSpec(memory_space=pltpu.SMEM)] + [pl.BlockSpec(memory_space=pl.ANY)] * 3,
        out_specs=vmem,
        scratch_shapes=[
            pltpu.VMEM(sources_in.shape, jnp.bfloat16),
            pltpu.VMEM(right.shape, jnp.bfloat16),
            pltpu.VMEM(left.shape, jnp.bfloat16),
            pltpu.VMEM((cols, width, 2 * CHUNK), jnp.bfloat16),
            pltpu.VMEM((n_row, depth, samples), jnp.bfloat16),
            pltpu.VMEM((n_row, depth, samples), jnp.bfloat16),
            pltpu.VMEM((n_row, 2 * width, depth), jnp.bfloat16),
            pltpu.VMEM((2 * width, CHUNK), jnp.float32),
            pltpu.VMEM((chunks, 2, share, CHUNK), jnp.float32),
            pltpu.VMEM((chunks, 2, width, CHUNK), jnp.bfloat16),
            pltpu.VMEM((chunks, n_col - 1, 2, share, CHUNK), jnp.bfloat16),
            pltpu.SemaphoreType.DMA((chunks + 3,)),
            pltpu.SemaphoreType.DMA((n_row, chunks)),
            pltpu.SemaphoreType.DMA((n_row, chunks)),
            pltpu.SemaphoreType.DMA((n_col, chunks)),
            pltpu.SemaphoreType.DMA((n_col, chunks)),
        ],
        compiler_params=pltpu.CompilerParams(
            collective_id=0, has_side_effects=True, vmem_limit_bytes=56 * 2**20
        ),
    )(tile_ranks.T, sources_in, right, left)


def solution(mesh):
    in_specs = (
        P(("row", "col"), None, None),
        P(("row", "col"), None, None, None, None),
        P("row", None, "col", None, None, None),
        P(None, ("row", "col")),
    )
    return jax.shard_map(
        functools.partial(body, mesh.shape["row"], mesh.shape["col"]),
        mesh=mesh,
        in_specs=in_specs,
        out_specs=P(("row", "col"), None, None),
        check_vma=False,
    )
```

```python
import functools

import jax
import jax.numpy as jnp
from jax import lax
from jax.experimental import pallas as pl
from jax.experimental.pallas import tpu as pltpu
from jax.sharding import PartitionSpec as P

MESH = pl.DeviceIdType.MESH
CHUNK = 128


def apply_kernel(
    n_row, n_col, ranks, sources, right, left_in, out, block, bases, left, split, coef, held,
    basis, total, own, outgoing, partial,
    load_sem, send_sem, recv_sem, psend_sem, precv_sem,
):
    row, col = lax.axis_index("row"), lax.axis_index("col")
    half = n_row // 2
    side = row // half
    place = row % half
    samples = coef.shape[2]
    tiles, _, rank_pad, width = left.shape
    cols = tiles // n_row
    chunks = samples // CHUNK
    share = width // n_col
    pair = 2 * rank_pad
    step_rows = 2 * CHUNK

    def load_part(ch):
        lanes = pl.ds(ch * CHUNK, CHUNK)
        return pltpu.make_async_copy(sources.at[:, :, lanes], block.at[:, :, lanes], load_sem.at[ch])

    def load_bases(there, at):
        span = pl.ds(there * half, half)
        return pltpu.make_async_copy(right.at[:, span], bases.at[:, span], load_sem.at[chunks + at])

    far_bases, near_bases = load_bases(1 - side, 0), load_bases(side, 1)
    load_left = pltpu.make_async_copy(left_in, left, load_sem.at[chunks + 2])
    load_part(0).start()
    far_bases.start()

    def to_row(k):
        far = k < half
        there = jnp.where(far, 1 - side, side)
        return there * half + (place + k) % half

    def from_row(k):
        far = k < half
        there = jnp.where(far, 1 - side, side)
        return there * half + (place + 2 * half - k) % half

    steps = [k for k in range(n_row) if k != half]

    barrier = pltpu.get_barrier_semaphore()
    for k in range(1, n_row):
        pl.semaphore_signal(barrier, inc=1, device_id={"row": (row + k) % n_row}, device_id_type=MESH)
    for k in range(1, n_col):
        pl.semaphore_signal(barrier, inc=1, device_id={"col": (col + k) % n_col}, device_id_type=MESH)

    def coef_copy(k, dest, slot, ch):
        lanes = pl.ds(ch * CHUNK, CHUNK)
        return pltpu.make_async_remote_copy(
            src_ref=coef.at[dest, :, lanes],
            dst_ref=held.at[slot, :, lanes],
            send_sem=send_sem.at[k, ch],
            recv_sem=recv_sem.at[k, ch],
            device_id={"row": dest},
            device_id_type=MESH,
        )

    at = lax.broadcasted_iota(jnp.int32, (step_rows, step_rows), 0)
    picked = jnp.where(at < CHUNK, 2 * at, 2 * (at - CHUNK) + 1)
    unweave = jnp.where(lax.broadcasted_iota(jnp.int32, (step_rows, step_rows), 1) == picked, 1.0, 0.0)
    unweave = unweave.astype(jnp.bfloat16)
    levels = lax.broadcasted_iota(jnp.int32, (rank_pad, CHUNK), 0)
    woven = block.reshape(2 * cols * width, samples)

    def project(dest, lanes):
        for c in range(cols):
            prod = jnp.dot(bases[c, dest], split[c], preferred_element_type=jnp.float32)
            real = prod[:rank_pad, :CHUNK] - prod[rank_pad:, CHUNK:]
            imag = prod[:rank_pad, CHUNK:] + prod[rank_pad:, :CHUNK]
            keep = levels < ranks[c, dest]
            coef[dest, c * pair : c * pair + rank_pad, lanes] = jnp.where(keep, real, 0.0).astype(coef.dtype)
            coef[dest, c * pair + rank_pad : (c + 1) * pair, lanes] = jnp.where(keep, imag, 0.0).astype(coef.dtype)

    for ch in range(chunks):
        lanes = pl.ds(ch * CHUNK, CHUNK)
        for c in range(cols):
            if c == 0:
                load_part(ch).wait()
            for t in range(width // CHUNK):
                rows = woven[pl.ds(2 * (c * width + t * CHUNK), step_rows), lanes]
                apart = jnp.dot(unweave, rows, preferred_element_type=jnp.float32).astype(split.dtype)
                split[c, t * CHUNK : (t + 1) * CHUNK, :CHUNK] = apart[:CHUNK]
                split[c, t * CHUNK : (t + 1) * CHUNK, CHUNK:] = apart[CHUNK:]
        if ch == 0:
            far_bases.wait()
            near_bases.start()
            for later in range(1, chunks):
                load_part(later).start()
            load_left.start()
            pl.semaphore_wait(barrier, n_row + n_col - 2)

        def project_send(k, carry):
            dest = to_row(k)
            project(dest, lanes)
            coef_copy(k, dest, row, ch).start()
            return carry

        lax.fori_loop(0, half, project_send, 0)
        if ch == 0:
            near_bases.wait()
        lax.fori_loop(half + 1, n_row, project_send, 0)
        project(row, lanes)
    load_left.wait()

    def prepare(a, carry):
        plain, swapped = [], []
        for c in range(cols):
            real, imag = left[a * cols + c, 0], left[a * cols + c, 1]
            plain += [real, -imag]
            swapped += [imag, real]
        basis[a, 0:width, :] = jnp.concatenate(plain, 0).T
        basis[a, width : 2 * width, :] = jnp.concatenate(swapped, 0).T
        return carry

    lax.fori_loop(0, n_row, prepare, 0)

    def partial_copy(k, ch):
        dest = (col + k) % n_col
        return pltpu.make_async_remote_copy(
            src_ref=outgoing.at[ch, :, pl.ds(pl.multiple_of(dest * share, share), share)],
            dst_ref=partial.at[ch, k - 1],
            send_sem=psend_sem.at[k, ch],
            recv_sem=precv_sem.at[k, ch],
            device_id={"col": dest},
            device_id_type=MESH,
        )

    to = lax.broadcasted_iota(jnp.int32, (2 * share, 2 * share), 0)
    near = lax.broadcasted_iota(jnp.int32, (2 * share, 2 * share), 1)
    weave = jnp.where(to == jnp.where(near < share, 2 * near, 2 * (near - share) + 1), 1.0, 0.0)
    weave = weave.astype(jnp.bfloat16)
    result = out.reshape(2 * share, samples)

    def finish(ch):
        mine = own[ch]
        for k in range(1, n_col):
            partial_copy(k, ch).wait_recv()
            mine = mine + partial[ch, k - 1].astype(jnp.float32)
        rounded = mine.astype(out.dtype).reshape(2 * share, CHUNK)
        woven_out = jnp.dot(weave, rounded, preferred_element_type=jnp.float32)
        result[:, pl.ds(ch * CHUNK, CHUNK)] = woven_out.astype(out.dtype)

    for ch in range(chunks):
        lanes = pl.ds(ch * CHUNK, CHUNK)
        total[...] = jnp.dot(basis[row], coef[row, :, lanes], preferred_element_type=jnp.float32)

        def take(k, carry):
            source = from_row(k)
            coef_copy(k, to_row(k), source, ch).wait_recv()
            total[...] += jnp.dot(basis[source], held[source, :, lanes], preferred_element_type=jnp.float32)
            return carry

        lax.fori_loop(half + 1, n_row, take, 0)
        lax.fori_loop(0, half, take, 0)
        outgoing[ch] = total[...].reshape(2, width, CHUNK).astype(outgoing.dtype)
        for q in range(2):
            own[ch, q] = total[pl.ds(pl.multiple_of(q * width + col * share, share), share)]
        for k in range(1, n_col):
            partial_copy(k, ch).start()
        if ch > 0:
            finish(ch - 1)
    finish(chunks - 1)
    for ch in range(chunks):
        for k in steps:
            coef_copy(k, to_row(k), row, ch).wait_send()
        for k in range(1, n_col):
            partial_copy(k, ch).wait_send()


def body(n_row, n_col, sources_in, right_bases, left_bases, tile_ranks):
    cols, tile_rows, _, rank_pad, width = right_bases.shape
    samples = sources_in.shape[2]
    depth = cols * 2 * rank_pad
    right = right_bases.reshape(cols, tile_rows, 2 * rank_pad, width)
    left = left_bases.reshape(-1, 2, rank_pad, width)
    chunks = samples // CHUNK
    share = width // n_col
    vmem = pl.BlockSpec(memory_space=pltpu.VMEM)
    scratch = [
        pltpu.VMEM(sources_in.shape, jnp.bfloat16),
        pltpu.VMEM(right.shape, jnp.bfloat16),
        pltpu.VMEM(left.shape, jnp.bfloat16),
        pltpu.VMEM((cols, width, 2 * CHUNK), jnp.bfloat16),
        pltpu.VMEM((n_row, depth, samples), jnp.bfloat16),
        pltpu.VMEM((n_row, depth, samples), jnp.bfloat16),
        pltpu.VMEM((n_row, 2 * width, depth), jnp.bfloat16),
        pltpu.VMEM((2 * width, CHUNK), jnp.float32),
        pltpu.VMEM((chunks, 2, share, CHUNK), jnp.float32),
        pltpu.VMEM((chunks, 2, width, CHUNK), jnp.bfloat16),
        pltpu.VMEM((chunks, n_col - 1, 2, share, CHUNK), jnp.bfloat16),
        pltpu.SemaphoreType.DMA((chunks + 3,)),
        pltpu.SemaphoreType.DMA((n_row, chunks)),
        pltpu.SemaphoreType.DMA((n_row, chunks)),
        pltpu.SemaphoreType.DMA((n_col, chunks)),
        pltpu.SemaphoreType.DMA((n_col, chunks)),
    ]
    held_bytes = sum(x.size * x.dtype.itemsize for x in (sources_in, right, left))
    held_bytes += n_row * depth * (2 * samples + 2 * width) * 2
    return pl.pallas_call(
        functools.partial(apply_kernel, n_row, n_col),
        out_shape=jax.ShapeDtypeStruct((share, 2, samples), jnp.bfloat16),
        in_specs=[pl.BlockSpec(memory_space=pltpu.SMEM)] + [pl.BlockSpec(memory_space=pltpu.HBM)] * 3,
        out_specs=vmem,
        scratch_shapes=scratch,
        compiler_params=pltpu.CompilerParams(
            collective_id=0, has_side_effects=True, vmem_limit_bytes=held_bytes + 12 * 2**20
        ),
    )(tile_ranks.T, *[pltpu.with_memory_space_constraint(x, pltpu.HBM) for x in (sources_in, right, left)])


def solution(mesh):
    in_specs = (
        P(("row", "col"), None, None),
        P(("row", "col"), None, None, None, None),
        P("row", None, "col", None, None, None),
        P(None, ("row", "col")),
    )
    return jax.shard_map(
        functools.partial(body, mesh.shape["row"], mesh.shape["col"]),
        mesh=mesh,
        in_specs=in_specs,
        out_specs=P(("row", "col"), None, None),
        check_vma=False,
    )
```
